512 devices in a mesh: dp: 16 (over z_hi, x, core), tensor: 32 (over z_lo, y).
Axes of the slice: x: 4, y: 8, z: 8 (z_hi: 2, z_lo: 4; z = z_hi * 4 + z_lo), core: 2. Of those that a mesh axis runs over, the one named last changes fastest.
Arguments:
- tokens: bfloat16 [8192, 4096], P(('dp', 'tensor')), parts along dimension 0, may hold values from -6 to 6
- norm_gain: float32 [4096], replicated, may hold values from 0.1 to 1.9
- gate_weight: bfloat16 [4096, 16384], P(None, 'tensor'), may hold values from -0.09375 to 0.09375
- up_weight: bfloat16 [4096, 16384], P(None, 'tensor'), may hold values from -0.09375 to 0.09375
- down_weight: bfloat16 [16384, 4096], P('tensor'), may hold values from -0.046875 to 0.046875
Outputs:
- mixed: bfloat16 [8192, 4096], P(('dp', 'tensor')), parts along dimension 0
The draws below stay inside these ranges and needn't reach their ends.
There are 16 independent parts, one for each index of `dp`. The reference program is written for one: setup_inputs(seed, part) draws one part's arguments, and reference() takes and returns one part's arrays. A program takes and returns all parts, laid end to end along the dimension named above; an argument that names none is the same for every part. Nothing has to cross between parts.
All inputs are finite; a program needn't handle non-finite values.
Results may differ from the reference program's by a relative error of at most 0.023.
Values may be sent and summed in bfloat16 or wider, within the bound.
A program may use at most 64 MiB of HBM per device.

```python
import jax
import jax.numpy as jnp
from jax import lax

D = 4096
FF = 16384
TOKENS = 512
N_TENSOR = 32


def level_of(stream_key, shape, pieces, low, high):
    def one(position, parts):
        heights = jax.random.uniform(jax.random.fold_in(jax.random.fold_in(stream_key, 6), position), (parts,), jnp.float32, low / len(pieces), high / len(pieces))
        return jnp.repeat(jnp.exp(heights), shape[position] // parts).reshape((-1,) + (1,) * (len(shape) - position - 1))

    factor_of = one(*pieces[0])
    for cut in pieces[1:]:
        factor_of = factor_of * one(*cut)
    return factor_of


def gaussian(rng, dims, width, most, pieces=(), dtype=jnp.bfloat16):
    drawn = jax.random.normal(rng, dims, jnp.float32) * width
    if len(pieces) > 0:
        drawn = level_of(rng, dims, pieces, -0.22, 0.18) * drawn
    return jnp.clip(drawn, min=-most, max=most).astype(dtype)


def setup_inputs(seed: int = 0, part: int = 0) -> dict:
    key_of = jax.random.split(jax.random.key(seed), 6)
    part_keys = jax.random.split(jax.random.fold_in(key_of[5], part), 6)
    tokens = gaussian(part_keys[0], (TOKENS, D), 1.0, 6.0, ((0, 32),))
    norm_gain = jnp.clip(1.0 + 0.18 * jax.random.normal(key_of[1], (D,), jnp.float32), 0.1, 1.9)
    gate_weight = gaussian(key_of[2], (D, FF), D ** -0.5, 0.09375, ((1, 32),))
    up_weight = gaussian(key_of[3], (D, FF), D ** -0.5, 0.09375, ((1, 32),))
    down_weight = gaussian(key_of[4], (FF, D), FF ** -0.5, 0.046875, ((0, 32),))
    return dict(tokens=tokens, norm_gain=norm_gain, gate_weight=gate_weight, up_weight=up_weight, down_weight=down_weight)


def reference(tokens, norm_gain, gate_weight, up_weight, down_weight):
    values = tokens.astype(jnp.float32)
    scale = lax.rsqrt(lax.optimization_barrier(jnp.mean(values * values, axis=1, keepdims=True)) + 1e-05)
    normed = (values * scale * norm_gain[None, :]).astype(jnp.bfloat16)
    gate = jnp.dot(normed, gate_weight, preferred_element_type=jnp.float32)
    up = jnp.dot(normed, up_weight, preferred_element_type=jnp.float32)
    hidden = (jax.nn.silu(gate) * up).astype(jnp.bfloat16)
    block = FF // N_TENSOR
    hidden_blocks = hidden.reshape(hidden.shape[0], N_TENSOR, block).transpose(1, 0, 2)
    down_blocks = down_weight.reshape(N_TENSOR, block, down_weight.shape[1])

    def accumulate(total, pair):
        part = jnp.dot(pair[0], pair[1], preferred_element_type=jnp.float32)
        return (total + part.astype(jnp.bfloat16).astype(jnp.float32), None)
    start = jnp.zeros((hidden.shape[0], down_weight.shape[1]), jnp.float32)
    total, unused = lax.scan(accumulate, start, (hidden_blocks, down_blocks))
    return total.astype(jnp.bfloat16)
```

```python
import jax
import jax.numpy as jnp
from jax import lax
from jax.experimental import pallas as pl
from jax.experimental.pallas import tpu as pltpu
from jax.sharding import PartitionSpec as P

NZ, NY = 4, 8
F32, BF16 = jnp.float32, jnp.bfloat16
HOPS = NY // 2
GA, GB, RA, RB = range(4)
CHAINS = [(half, way) for half in (0, 1) for way in (0, 1)]


def kernel(
    tokens, gain, gate_hbm, up_hbm, down_hbm, out,
    xa, xb, pa, pb, hidden, gate_w, up_w, down_w,
    ring_a, ring_b, line_a, line_b,
    load_sem, ring_send, ring_recv, line_send, line_recv,
):
    me = lax.axis_index("tensor")
    z, y = me // NY, me % NY
    ca, cb = xa.shape[-1], xb.shape[-1]
    rows = tokens.shape[0]
    width = hidden.shape[-1]

    loads = [
        pltpu.make_async_copy(src, dst, load_sem.at[i])
        for i, (src, dst) in enumerate(((gate_hbm, gate_w), (up_hbm, up_w), (down_hbm, down_w)))
    ]
    for load in loads:
        load.start()

    def ring_next(way):
        return z * NY + (y + (1 if way else NY - 1)) % NY

    barrier = pltpu.get_barrier_semaphore()
    for way in (0, 1):
        pl.semaphore_signal(barrier, inc=1, device_id={"tensor": ring_next(way)})

    @pl.when(z > 0)
    def _():
        pl.semaphore_signal(barrier, inc=1, device_id={"tensor": me - NY})

    @pl.when(z < NZ - 1)
    def _():
        pl.semaphore_signal(barrier, inc=1, device_id={"tensor": me + NY})

    values = tokens[...].astype(F32)
    scale = lax.rsqrt(jnp.mean(values * values, axis=1, keepdims=True) + 1e-05)
    normed = (values * scale * gain[...]).astype(BF16)
    xa[z, y] = normed[:, :ca]
    xb[z, y] = normed[:, ca:]

    inside = (z > 0).astype(jnp.int32) + (z < NZ - 1).astype(jnp.int32)
    pl.semaphore_wait(barrier, 2 + inside)

    def cols(ref, half):
        c = ref.shape[-1] // 2
        return pl.ds(half * c, c)

    def region_ra(ref):
        return lambda yi, half: ref.at[:, yi, :, cols(ref, half)]

    def region_rb(ref):
        return lambda yi, half: ref.at[z, yi, :, cols(ref, half)]

    def region_la(ref):
        return lambda zi: ref.at[zi, y]

    def region_lb(ref):
        return lambda zi: ref.at[zi]

    def length(half, way):
        return HOPS if half == way else HOPS - 1

    def ring_copy(use, half, way, s, src, dst):
        return pltpu.make_async_remote_copy(
            src_ref=src, dst_ref=dst,
            send_sem=ring_send.at[use, half, way, s],
            recv_sem=ring_recv.at[use, half, way, s],
            device_id={"tensor": ring_next(way)},
        )

    def line_copy(use, way, s, src, dst):
        return pltpu.make_async_remote_copy(
            src_ref=src, dst_ref=dst,
            send_sem=line_send.at[use, way, s],
            recv_sem=line_recv.at[use, way, s],
            device_id={"tensor": me + (NY if way else -NY)},
        )

    def gather_ring(use, region):
        def block(way, s):
            return (y + (NY - s if way else s)) % NY

        def start(s):
            for half, way in CHAINS:
                if s < length(half, way):
                    ref = region(block(way, s), half)
                    ring_copy(use, half, way, s, ref, ref).start()

        def recv(s):
            for half, way in CHAINS:
                if s < length(half, way):
                    ref = region(block(way, s + 1), half)
                    ring_copy(use, half, way, s, ref, ref).wait_recv()

        def done():
            for half, way in CHAINS:
                for s in range(length(half, way)):
                    ref = region(block(way, s), half)
                    ring_copy(use, half, way, s, ref, ref).wait_send()

        return start, recv, done

    def rank(way):
        return z if way else NZ - 1 - z

    def place(way, q):
        return q if way else NZ - 1 - q

    def gather_line(use, region):
        def sends(way, s, act):
            q = rank(way)

            @pl.when((q >= s) & (q < NZ - 1))
            def _():
                ref = region(place(way, q - s))
                act(line_copy(use, way, s, ref, ref))

        def start(s):
            for way in (0, 1):
                sends(way, s, lambda c: c.start())

        def recv(s):
            for way in (0, 1):
                q = rank(way)

                @pl.when(q >= s + 1)
                def _():
                    ref = region(place(way, q - 1 - s))
                    line_copy(use, way, s, ref, ref).wait_recv()

        def done():
            for way in (0, 1):
                for s in range(NZ - 1):
                    sends(way, s, lambda c: c.wait_send())

        return start, recv, done

    def add(dst, src):
        dst[...] = (dst[...].astype(F32) + src[...].astype(F32)).astype(BF16)

    def scatter_ring(use, region, slots):
        def block(way, s):
            return (y + (HOPS - s if way else NY - HOPS + s)) % NY

        def first(half, way):
            return HOPS - length(half, way)

        def step(s):
            for half, way in CHAINS:
                f = first(half, way)
                if s < f:
                    continue
                ref = region(block(way, s), half)
                if s > f:
                    slot = slots.at[half, way, s - 1]
                    ring_copy(use, half, way, s - 1, slot, slot).wait_recv()
                    add(ref, slot)
                ring_copy(use, half, way, s, ref, slots.at[half, way, s]).start()

        def finish():
            for half, way in CHAINS:
                slot = slots.at[half, way, HOPS - 1]
                ring_copy(use, half, way, HOPS - 1, slot, slot).wait_recv()
                add(region(y, half), slot)

        def done():
            for half, way in CHAINS:
                for s in range(first(half, way), HOPS):
                    ref = region(block(way, s), half)
                    ring_copy(use, half, way, s, ref, slots.at[half, way, s]).wait_send()

        return step, finish, done

    def scatter_line(use, region, slots):
        last = NZ - 2

        def step(s):
            for way in (0, 1):
                q = rank(way)
                ref = region(place(way, NZ - 1 + q - s))
                if s > 0:

                    @pl.when((q >= 1) & (q <= s))
                    def _():
                        slot = slots.at[way, s - 1]
                        line_copy(use, way, s - 1, slot, slot).wait_recv()
                        add(ref, slot)

                @pl.when(q <= s)
                def _():
                    line_copy(use, way, s, ref, slots.at[way, s]).start()

        def finish():
            for way in (0, 1):

                @pl.when(rank(way) >= 1)
                def _():
                    slot = slots.at[way, last]
                    line_copy(use, way, last, slot, slot).wait_recv()
                    add(region(z), slot)

        def done():
            for way in (0, 1):
                for s in range(NZ - 1):
                    q = rank(way)

                    @pl.when(q <= s)
                    def _():
                        ref = region(place(way, NZ - 1 + q - s))
                        line_copy(use, way, s, ref, slots.at[way, s]).wait_send()

        return step, finish, done

    gla, gra = gather_line(GA, region_la(xa)), gather_ring(GA, region_ra(xa))
    grb, glb = gather_ring(GB, region_rb(xb)), gather_line(GB, region_lb(xb))
    gla[0](0)
    grb[0](0)
    for s in range(NZ - 1):
        gla[1](s)
        if s < NZ - 2:
            gla[0](s + 1)
        else:
            gra[0](0)
        grb[1](s)
        grb[0](s + 1)
    grb[1](HOPS - 1)
    glb[0](0)
    for s in range(HOPS):
        gra[1](s)
        if s < HOPS - 1:
            gra[0](s + 1)
        if s < NZ - 1:
            glb[1](s)
            if s < NZ - 2:
                glb[0](s + 1)
    for load in loads:
        load.wait()

    tile = min(256, width)
    deep = 2 * NY * rows

    def up_project(i, carry):
        m, n = i % 2, i // 2
        at = pl.ds(pl.multiple_of(n * tile, tile), tile)
        part = pl.ds(2 * m, 2)
        left, right = xa[part].reshape(deep, ca), xb[part].reshape(deep, cb)

        def dot(w):
            return jnp.dot(left, w[:ca, at], preferred_element_type=F32) + jnp.dot(
                right, w[ca:, at], preferred_element_type=F32
            )

        gate = dot(gate_w)
        h = gate / (1.0 + jnp.exp(-gate)) * dot(up_w)
        hidden[part, :, :, at] = h.astype(BF16).reshape(2, NY, rows, tile)
        return carry

    lax.fori_loop(0, 2 * (width // tile), up_project, 0)

    tile_a, tile_b = ca // 2, cb // 2

    def down_a(yi):
        h = hidden[:, yi].reshape(NZ * rows, width)

        def body(n, carry):
            at = pl.ds(pl.multiple_of(n * tile_a, 128), tile_a)
            part = jnp.dot(h, down_w[:, at], preferred_element_type=F32)
            pa[:, yi, :, at] = part.astype(BF16).reshape(NZ, rows, tile_a)
            return carry

        lax.fori_loop(0, 2, body, 0)

    def down_b(i, carry):
        zi, n = i // 2, i % 2
        h = hidden[zi].reshape(NY * rows, width)
        w_at = pl.ds(pl.multiple_of(ca + n * tile_b, 128), tile_b)
        at = pl.ds(pl.multiple_of(n * tile_b, 128), tile_b)
        part = jnp.dot(h, down_w[:, w_at], preferred_element_type=F32)
        pb[zi, :, :, at] = part.astype(BF16).reshape(NY, rows, tile_b)
        return carry

    sra, sla = scatter_ring(RA, region_ra(pa), ring_a), scatter_line(RA, region_la(pa), line_a)
    slb, srb = scatter_line(RB, region_lb(pb), line_b), scatter_ring(RB, region_rb(pb), ring_b)
    down_a((y + HOPS) % NY)
    sra[0](0)
    lax.fori_loop(0, 2 * NZ, down_b, 0)
    slb[0](0)
    for s in range(1, HOPS):
        down_a((y + HOPS - s) % NY)
        down_a((y + HOPS + s) % NY)
        if s == 1:
            down_a(y)
        sra[0](s)
        if s < NZ - 1:
            slb[0](s)
    slb[1]()
    srb[0](0)
    sra[1]()
    sla[0](0)
    for s in range(1, HOPS):
        srb[0](s)
        if s < NZ - 1:
            sla[0](s)
    sla[1]()
    srb[1]()
    out[:, :ca] = pa[z, y]
    out[:, ca:] = pb[z, y]
    for part in (gla, gra, grb, glb, sra, sla, slb, srb):
        part[2]()


def on_device(tokens, norm_gain, gate_weight, up_weight, down_weight):
    rows, d = tokens.shape
    width = gate_weight.shape[1]
    ca = d // 8 * 5
    cb = d - ca
    vmem, anywhere = (pl.BlockSpec(memory_space=space) for space in (pltpu.VMEM, pl.ANY))
    dma = pltpu.SemaphoreType.DMA
    return pl.pallas_call(
        kernel,
        out_shape=jax.ShapeDtypeStruct((rows, d), BF16),
        in_specs=[vmem, vmem, anywhere, anywhere, anywhere],
        out_specs=vmem,
        scratch_shapes=[
            pltpu.VMEM((NZ, NY, rows, ca), BF16),
            pltpu.VMEM((NZ, NY, rows, cb), BF16),
            pltpu.VMEM((NZ, NY, rows, ca), BF16),
            pltpu.VMEM((NZ, NY, rows, cb), BF16),
            pltpu.VMEM((NZ, NY, rows, width), BF16),
            pltpu.VMEM((d, width), BF16),
            pltpu.VMEM((d, width), BF16),
            pltpu.VMEM((width, d), BF16),
            pltpu.VMEM((2, 2, HOPS, NZ, rows, ca // 2), BF16),
            pltpu.VMEM((2, 2, HOPS, rows, cb // 2), BF16),
            pltpu.VMEM((2, NZ - 1, rows, ca), BF16),
            pltpu.VMEM((2, NZ - 1, NY, rows, cb), BF16),
            dma((3,)),
            dma((4, 2, 2, HOPS)),
            dma((4, 2, 2, HOPS)),
            dma((4, 2, NZ - 1)),
            dma((4, 2, NZ - 1)),
        ],
        compiler_params=pltpu.CompilerParams(
            collective_id=0, has_side_effects=True, vmem_limit_bytes=60 * 1024 * 1024
        ),
    )(tokens, norm_gain.reshape(1, d), gate_weight, up_weight, down_weight)


def solution(mesh):
    return jax.shard_map(
        on_device,
        mesh=mesh,
        in_specs=(
            P(("dp", "tensor"), None),
            P(),
            P(None, "tensor"),
            P(None, "tensor"),
            P("tensor", None),
        ),
        out_specs=P(("dp", "tensor"), None),
        check_vma=False,
    )
```

```python
import functools

import jax
import jax.numpy as jnp
from jax import lax
from jax.experimental import pallas as pl
from jax.experimental.pallas import tpu as pltpu
from jax.sharding import PartitionSpec as P

NZ = 4
F32, BF16 = jnp.float32, jnp.bfloat16
GA, GB, RA, RB = range(4)
FAR, RELAY, NEAR = range(3)
CHAINS = [(half, way) for half in (0, 1) for way in (0, 1)]


def kernel(
    n_dp, ny,
    tokens, gain, gate_hbm, up_hbm, down_hbm, out,
    xa, xb, pa, pb, acc, hidden, gate_w, up_w, down_w,
    ring_a, ring_b, line_a, line_b,
    load_sem, ring_send, ring_recv, line_send, line_recv,
):
    me, dp = lax.axis_index("tensor"), lax.axis_index("dp")
    z, y = me // ny, me % ny
    hops = ny // 2
    upper = n_dp // 2
    z_all = dp // upper * NZ + z
    turn = 1 - 2 * (dp % 2)
    ca, cb = xa.shape[-1], xb.shape[-1]
    rows = tokens.shape[0]
    width = hidden.shape[-1]

    loads = [
        pltpu.make_async_copy(src, dst, load_sem.at[i])
        for i, (src, dst) in enumerate(((gate_hbm, gate_w), (up_hbm, up_w), (down_hbm, down_w)))
    ]
    for load in loads:
        load.start()

    def ring_next(way):
        return {"dp": dp, "tensor": z * ny + (y + (1 if way else ny - 1)) % ny}

    def line_next(ahead):
        to = (z_all + 2 * NZ + (turn if ahead else -turn)) % (2 * NZ)
        return {"dp": dp % upper + to // NZ * upper, "tensor": to % NZ * ny + y}

    barrier = pltpu.get_barrier_semaphore()
    for way in (0, 1):
        pl.semaphore_signal(barrier, inc=1, device_id=ring_next(way))
        pl.semaphore_signal(barrier, inc=1, device_id=line_next(way))

    values = tokens[...].astype(F32)
    scale = lax.rsqrt(jnp.mean(values * values, axis=1, keepdims=True) + 1e-05)
    normed = (values * scale * gain[...]).astype(BF16)
    xa[0, y] = normed[:, :ca]
    xb[0, y] = normed[:, ca:]

    pl.semaphore_wait(barrier, 4)

    def cols(ref, half):
        c = ref.shape[-1] // 2
        return pl.ds(half * c, c)

    def region_ra(ref):
        return lambda yi, half: ref.at[:, yi, :, cols(ref, half)]

    def region_rb(ref):
        return lambda yi, half: ref.at[0, yi, :, cols(ref, half)]

    def region_la(ref):
        return lambda slot, piece: ref.at[slot, y]

    def region_lb(ref):
        return lambda slot, piece: ref.at[slot, pl.ds(piece * hops, hops)]

    def length(half, way):
        return hops if half == way else hops - 1

    def ring_copy(use, half, way, s, src, dst):
        return pltpu.make_async_remote_copy(
            src_ref=src, dst_ref=dst,
            send_sem=ring_send.at[use, half, way, s],
            recv_sem=ring_recv.at[use, half, way, s],
            device_id=ring_next(way),
        )

    def line_copy(use, kind, piece, ahead, src, dst):
        return pltpu.make_async_remote_copy(
            src_ref=src, dst_ref=dst,
            send_sem=line_send.at[use, kind, piece],
            recv_sem=line_recv.at[use, kind, piece],
            device_id=line_next(ahead),
        )

    def gather_ring(use, region):
        def block(way, s):
            return (y + (ny - s if way else s)) % ny

        def start(s):
            for half, way in CHAINS:
                if s < length(half, way):
                    ref = region(block(way, s), half)
                    ring_copy(use, half, way, s, ref, ref).start()

        def recv(s):
            for half, way in CHAINS:
                if s < length(half, way):
                    ref = region(block(way, s + 1), half)
                    ring_copy(use, half, way, s, ref, ref).wait_recv()

        def done():
            for half, way in CHAINS:
                for s in range(length(half, way)):
                    ref = region(block(way, s), half)
                    ring_copy(use, half, way, s, ref, ref).wait_send()

        return start, recv, done

    def gather_line(use, region):
        def copy(kind, piece):
            src, dst = {FAR: (0, 1), RELAY: (1, 2), NEAR: (0, 3)}[kind]
            return line_copy(use, kind, piece, kind != NEAR, region(src, piece), region(dst, piece))

        return copy

    def scatter_line(use, region, slots):
        def copy(kind, piece):
            src = {FAR: 2, RELAY: 1, NEAR: 3}[kind]
            dst = region_of(slots, kind, piece)
            return line_copy(use, kind, piece, kind == NEAR, region(src, piece), dst)

        def region_of(ref, kind, piece):
            return ref.at[kind] if use == RA else ref.at[kind, pl.ds(piece * hops, hops)]

        def relay(piece):
            copy(FAR, piece).wait_recv()
            add(region(1, piece), region_of(slots, FAR, piece))
            copy(RELAY, piece).start()

        def finish(piece):
            for kind in (NEAR, RELAY):
                copy(kind, piece).wait_recv()
                add(region(0, piece), region_of(slots, kind, piece))

        return copy, relay, finish

    def add(dst, src):
        dst[...] = (dst[...].astype(F32) + src[...].astype(F32)).astype(BF16)

    def scatter_ring(use, region, slots):
        def block(way, s):
            return (y + (hops - s if way else ny - hops + s)) % ny

        def first(half, way):
            return hops - length(half, way)

        def step(s):
            for half, way in CHAINS:
                f = first(half, way)
                if s < f:
                    continue
                ref = region(block(way, s), half)
                if s > f:
                    slot = slots.at[half, way, s - 1]
                    ring_copy(use, half, way, s - 1, slot, slot).wait_recv()
                    add(ref, slot)
                ring_copy(use, half, way, s, ref, slots.at[half, way, s]).start()

        def finish():
            for half, way in CHAINS:
                slot = slots.at[half, way, hops - 1]
                ring_copy(use, half, way, hops - 1, slot, slot).wait_recv()
                add(region(y, half), slot)

        def done():
            for half, way in CHAINS:
                for s in range(first(half, way), hops):
                    ref = region(block(way, s), half)
                    ring_copy(use, half, way, s, ref, slots.at[half, way, s]).wait_send()

        return step, finish, done

    gla, gra = gather_line(GA, region_la(xa)), gather_ring(GA, region_ra(xa))
    grb, glb = gather_ring(GB, region_rb(xb)), gather_line(GB, region_lb(xb))
    gla(FAR, 0).start()
    gla(NEAR, 0).start()
    grb[0](0)
    acc[...] = jnp.zeros_like(acc)
    gla(FAR, 0).wait_recv()
    gla(RELAY, 0).start()
    grb[1](0)
    grb[0](1)
    gla(NEAR, 0).wait_recv()
    gla(RELAY, 0).wait_recv()
    gra[0](0)
    for s in range(1, hops):
        grb[1](s)
        if s < hops - 1:
            grb[0](s + 1)
    for piece in (0, 1):
        glb(FAR, piece).start()
    for piece in (0, 1):
        glb(NEAR, piece).start()

    tile = min(256, width)

    def up_project(load, lo, size, store):
        def body(n, carry):
            at = pl.ds(pl.multiple_of(n * tile, tile), tile)
            left = load()
            for i, w in enumerate((gate_w, up_w)):
                store(i, at, jnp.dot(left, w[lo : lo + size, at], preferred_element_type=F32))
            return carry

        lax.fori_loop(0, width // tile, body, 0)

    def up_a(*groups):
        def load():
            return jnp.concatenate([xa[:, yi].reshape(NZ * rows, ca) for yi in groups], axis=0)

        def store(i, at, part):
            parts = part.reshape(len(groups), NZ, rows, tile)
            for g, yi in enumerate(groups):
                acc[i, :, yi, :, at] += parts[g]

        up_project(load, 0, ca, store)

    def up_b(slot):
        def store(i, at, part):
            acc[i, slot, :, :, at] += part.reshape(ny, rows, tile)

        up_project(lambda: xb[slot].reshape(ny * rows, cb), ca, cb, store)

    loads[0].wait()
    loads[1].wait()
    up_a(y)
    for s in range(hops):
        gra[1](s)
        if s < hops - 1:
            gra[0](s + 1)
        if s >= hops - 3 and s < hops - 1:
            piece = s - (hops - 3)
            glb(FAR, piece).wait_recv()
            glb(RELAY, piece).start()
        if s < hops - 1:
            up_a((y + s + 1) % ny, (y + ny - s - 1) % ny)
        if s == 0:
            up_b(0)
        if s == hops - 2:
            up_b(1)
    for piece in (0, 1):
        glb(NEAR, piece).wait_recv()
    up_a((y + hops) % ny)
    up_b(3)
    for piece in (0, 1):
        glb(RELAY, piece).wait_recv()
    up_b(2)

    def activate(i, carry):
        gate, up = acc[0, i // ny, i % ny], acc[1, i // ny, i % ny]
        hidden[i // ny, i % ny] = (gate / (1.0 + jnp.exp(-gate)) * up).astype(BF16)
        return carry

    lax.fori_loop(0, NZ * ny, activate, 0, unroll=4)
    loads[2].wait()
    tile_a, tile_b = ca // 2, cb // 2

    def down_a(yi):
        h = hidden[:, yi].reshape(NZ * rows, width)

        def body(n, carry):
            at = pl.ds(pl.multiple_of(n * tile_a, 128), tile_a)
            part = jnp.dot(h, down_w[:, at], preferred_element_type=F32)
            pa[:, yi, :, at] = part.astype(BF16).reshape(NZ, rows, tile_a)
            return carry

        lax.fori_loop(0, 2, body, 0)

    def down_b(slot):
        h = hidden[slot].reshape(ny * rows, width)

        def body(n, carry):
            w_at = pl.ds(pl.multiple_of(ca + n * tile_b, 128), tile_b)
            at = pl.ds(pl.multiple_of(n * tile_b, 128), tile_b)
            part = jnp.dot(h, down_w[:, w_at], preferred_element_type=F32)
            pb[slot, :, :, at] = part.astype(BF16).reshape(ny, rows, tile_b)
            return carry

        lax.fori_loop(0, 2, body, 0)

    sra, sla = scatter_ring(RA, region_ra(pa), ring_a), scatter_line(RA, region_la(pa), line_a)
    slb, srb = scatter_line(RB, region_lb(pb), line_b), scatter_ring(RB, region_rb(pb), ring_b)
    down_a((y + hops) % ny)
    sra[0](0)
    for slot, kind in ((2, FAR), (3, NEAR)):
        down_b(slot)
        for piece in (0, 1):
            slb[0](kind, piece).start()
    down_b(1)
    for s in range(1, hops):
        down_a((y + hops - s) % ny)
        down_a((y + hops + s) % ny)
        if s == 1:
            down_b(0)
        if s == hops - 1:
            down_a(y)
        sra[0](s)
        if s >= hops - 3 and s < hops - 1:
            slb[1](s - (hops - 3))
    sra[1]()
    sla[0](FAR, 0).start()
    sla[0](NEAR, 0).start()
    for piece in (0, 1):
        slb[2](piece)
    srb[0](0)
    sla[1](0)
    for s in range(1, hops):
        srb[0](s)
    sla[2](0)
    srb[1]()
    out[:, :ca] = pa[0, y]
    out[:, ca:] = pb[0, y]
    for kind in (FAR, RELAY, NEAR):
        gla(kind, 0).wait_send()
        sla[0](kind, 0).wait_send()
        for piece in (0, 1):
            glb(kind, piece).wait_send()
            slb[0](kind, piece).wait_send()
    for part in (gra, grb, sra, srb):
        part[2]()


def on_device(n_dp, n_tensor, tokens, norm_gain, gate_weight, up_weight, down_weight):
    rows, d = tokens.shape
    width = gate_weight.shape[1]
    ny = n_tensor // NZ
    hops = ny // 2
    ca = d // 16 * 7
    cb = d - ca
    vmem, anywhere = (pl.BlockSpec(memory_space=space) for space in (pltpu.VMEM, pl.ANY))
    dma = pltpu.SemaphoreType.DMA
    return pl.pallas_call(
        functools.partial(kernel, n_dp, ny),
        out_shape=jax.ShapeDtypeStruct((rows, d), BF16),
        in_specs=[vmem, vmem, anywhere, anywhere, anywhere],
        out_specs=vmem,
        scratch_shapes=[
            pltpu.VMEM((NZ, ny, rows, ca), BF16),
            pltpu.VMEM((NZ, ny, rows, cb), BF16),
            pltpu.VMEM((NZ, ny, rows, ca), BF16),
            pltpu.VMEM((NZ, ny, rows, cb), BF16),
            pltpu.VMEM((2, NZ, ny, rows, width), F32),
            pltpu.VMEM((NZ, ny, rows, width), BF16),
            pltpu.VMEM((d, width), BF16),
            pltpu.VMEM((d, width), BF16),
            pltpu.VMEM((width, d), BF16),
            pltpu.VMEM((2, 2, hops, NZ, rows, ca // 2), BF16),
            pltpu.VMEM((2, 2, hops, rows, cb // 2), BF16),
            pltpu.VMEM((3, rows, ca), BF16),
            pltpu.VMEM((3, ny, rows, cb), BF16),
            dma((3,)),
            dma((4, 2, 2, hops)),
            dma((4, 2, 2, hops)),
            dma((4, 3, 2)),
            dma((4, 3, 2)),
        ],
        compiler_params=pltpu.CompilerParams(
            collective_id=0, has_side_effects=True, vmem_limit_bytes=60 * 1024 * 1024
        ),
    )(tokens, norm_gain.reshape(1, d), gate_weight, up_weight, down_weight)


def solution(mesh):
    return jax.shard_map(
        functools.partial(on_device, mesh.shape["dp"], mesh.shape["tensor"]),
        mesh=mesh,
        in_specs=(
            P(("dp", "tensor"), None),
            P(),
            P(None, "tensor"),
            P(None, "tensor"),
            P("tensor", None),
        ),
        out_specs=P(("dp", "tensor"), None),
        check_vma=False,
    )
```

```python
import functools

import jax
import jax.numpy as jnp
from jax import lax
from jax.experimental import pallas as pl
from jax.experimental.pallas import tpu as pltpu
from jax.sharding import PartitionSpec as P

NZ = 4
F32, BF16 = jnp.float32, jnp.bfloat16
GA, GB, RA, RB = 0, 4, 5, 9
LGA, LGB, LRA, LRB = range(4)
FAR, RELAY, NEAR = range(3)
CHAINS = [(half, way) for half in (0, 1) for way in (0, 1)]


def kernel(
    n_dp, ny,
    tokens, gain, gate_hbm, up_hbm, down_hbm, out,
    xa, xb, pa, pb, hidden, gate_w, up_w, down_w,
    ring_a, ring_b, line_a, line_b,
    load_sem, ring_send, ring_recv, line_send, line_recv,
):
    me, dp = lax.axis_index("tensor"), lax.axis_index("dp")
    z, y = me // ny, me % ny
    hops = ny // 2
    upper = n_dp // 2
    z_all = dp // upper * NZ + z
    turn = 1 - 2 * (dp % 2)
    ca, cb = xa.shape[-1], xb.shape[-1]
    rows = tokens.shape[0]
    width = hidden.shape[-1]

    loads = [
        pltpu.make_async_copy(src, dst, load_sem.at[i])
        for i, (src, dst) in enumerate(((gate_hbm, gate_w), (up_hbm, up_w), (down_hbm, down_w)))
    ]
    for load in loads:
        load.start()

    def ring_next(way):
        return {"dp": dp, "tensor": z * ny + (y + (1 if way else ny - 1)) % ny}

    def line_next(ahead):
        to = (z_all + 2 * NZ + (turn if ahead else -turn)) % (2 * NZ)
        return {"dp": dp % upper + to // NZ * upper, "tensor": to % NZ * ny + y}

    barrier = pltpu.get_barrier_semaphore()
    for way in (0, 1):
        pl.semaphore_signal(barrier, inc=1, device_id=ring_next(way))
        pl.semaphore_signal(barrier, inc=1, device_id=line_next(way))

    values = tokens[...].astype(F32)
    scale = lax.rsqrt(jnp.mean(values * values, axis=1, keepdims=True) + 1e-05)
    normed = (values * scale * gain[...]).astype(BF16)
    xa[0, y] = normed[:, :ca]
    xb[0, y] = normed[:, ca:]

    pl.semaphore_wait(barrier, 4)

    def cols(ref, half):
        c = ref.shape[-1] // 2
        return pl.ds(half * c, c)

    def on_ring(ref, slot):
        return lambda yi, half: ref.at[slot, yi, :, cols(ref, half)]

    def near_y(d):
        return [(y + e) % ny for e in sorted({d, (ny - d) % ny}, reverse=True)]

    def pieces(d):
        return [(2 * d - 1 + i if d else 0, yi) for i, yi in enumerate(near_y(d))]

    def length(half, way):
        return hops if half == way else hops - 1

    def ring_copy(use, half, way, s, src, dst):
        return pltpu.make_async_remote_copy(
            src_ref=src, dst_ref=dst,
            send_sem=ring_send.at[use, half, way, s],
            recv_sem=ring_recv.at[use, half, way, s],
            device_id=ring_next(way),
        )

    def line_copy(use, kind, piece, ahead, src, dst):
        return pltpu.make_async_remote_copy(
            src_ref=src, dst_ref=dst,
            send_sem=line_send.at[use, kind, piece],
            recv_sem=line_recv.at[use, kind, piece],
            device_id=line_next(ahead),
        )

    def gather_ring(use, region):
        def block(way, s):
            return (y + (ny - s if way else s)) % ny

        def start(s):
            for half, way in CHAINS:
                if s < length(half, way):
                    ref = region(block(way, s), half)
                    ring_copy(use, half, way, s, ref, ref).start()

        def recv(s):
            for half, way in CHAINS:
                if s < length(half, way):
                    ref = region(block(way, s + 1), half)
                    ring_copy(use, half, way, s, ref, ref).wait_recv()

        def done():
            for half, way in CHAINS:
                for s in range(length(half, way)):
                    ref = region(block(way, s), half)
                    ring_copy(use, half, way, s, ref, ref).wait_send()

        return start, recv, done

    def gather_line(use, ref):
        def copy(kind, piece, yi):
            src, dst = {FAR: (0, 1), RELAY: (1, 2), NEAR: (0, 3)}[kind]
            return line_copy(use, kind, piece, kind != NEAR, ref.at[src, yi], ref.at[dst, yi])

        return copy

    def scatter_line(use, ref, slots):
        def copy(kind, piece, yi):
            src = {FAR: 2, RELAY: 1, NEAR: 3}[kind]
            return line_copy(use, kind, piece, kind == NEAR, ref.at[src, yi], slots.at[kind, piece])

        def relay(piece, yi):
            copy(FAR, piece, yi).wait_recv()
            add(ref.at[1, yi], slots.at[FAR, piece])
            copy(RELAY, piece, yi).start()

        def finish(piece, yi):
            for kind in (NEAR, RELAY):
                copy(kind, piece, yi).wait_recv()
                add(ref.at[0, yi], slots.at[kind, piece])

        return copy, relay, finish

    def add(dst, src):
        dst[...] = (dst[...].astype(F32) + src[...].astype(F32)).astype(BF16)

    def scatter_ring(use, region, slots):
        def block(way, s):
            return (y + (hops - s if way else ny - hops + s)) % ny

        def first(half, way):
            return hops - length(half, way)

        def step(s):
            for half, way in CHAINS:
                f = first(half, way)
                if s < f:
                    continue
                ref = region(block(way, s), half)
                if s > f:
                    slot = slots.at[half, way, s - 1]
                    ring_copy(use, half, way, s - 1, slot, slot).wait_recv()
                    add(ref, slot)
                ring_copy(use, half, way, s, ref, slots.at[half, way, s]).start()

        def finish():
            for half, way in CHAINS:
                slot = slots.at[half, way, hops - 1]
                ring_copy(use, half, way, hops - 1, slot, slot).wait_recv()
                add(region(y, half), slot)

        def done():
            for half, way in CHAINS:
                for s in range(first(half, way), hops):
                    ref = region(block(way, s), half)
                    ring_copy(use, half, way, s, ref, slots.at[half, way, s]).wait_send()

        return step, finish, done

    tile = min(256, width)

    def up_project(d):
        groups = near_y(d)
        deep = len(groups) * NZ * rows

        def body(n, carry):
            at = pl.ds(pl.multiple_of(n * tile, tile), tile)
            left, right = (
                jnp.concatenate([x[:, yi].reshape(NZ * rows, x.shape[-1]) for yi in groups], axis=0)
                for x in (xa, xb)
            )

            def dot(w):
                return jnp.dot(left, w[:ca, at], preferred_element_type=F32) + jnp.dot(
                    right, w[ca:, at], preferred_element_type=F32
                )

            gate = dot(gate_w)
            h = (gate / (1.0 + jnp.exp(-gate)) * dot(up_w)).astype(BF16)
            h = h.reshape(len(groups), NZ, rows, tile)
            for g, yi in enumerate(groups):
                hidden[:, yi, :, at] = h[g]
            return carry

        lax.fori_loop(0, width // tile, body, 0)

    gla, glb = gather_line(LGA, xa), gather_line(LGB, xb)
    gra = [gather_ring(GA + slot, on_ring(xa, slot)) for slot in range(NZ)]
    grb = gather_ring(GB, on_ring(xb, 0))
    begins = (0, 1, 2, 1)

    def ring_tick(ring, t):
        if 0 < t <= hops:
            ring[1](t - 1)
        if 0 <= t < hops:
            ring[0](t)

    for t in range(hops + 3):
        if t == 0:
            gla(FAR, 0, y).start()
            gla(NEAR, 0, y).start()
        if t == 1:
            gla(FAR, 0, y).wait_recv()
            gla(RELAY, 0, y).start()
            gla(NEAR, 0, y).wait_recv()
        if t == 2:
            gla(RELAY, 0, y).wait_recv()
        ring_tick(grb, t)
        if t <= hops:
            for piece, yi in pieces(t):
                glb(FAR, piece, yi).start()
        if 1 <= t <= hops + 1:
            for piece, yi in pieces(t - 1):
                glb(FAR, piece, yi).wait_recv()
                glb(RELAY, piece, yi).start()
        if t <= hops:
            for piece, yi in pieces(t):
                glb(NEAR, piece, yi).start()
        for slot in (0, 1, 3, 2):
            ring_tick(gra[slot], t - begins[slot])
        if t == 2:
            loads[0].wait()
            loads[1].wait()
        if t >= 2:
            for piece, yi in pieces(t - 2):
                glb(NEAR, piece, yi).wait_recv()
                glb(RELAY, piece, yi).wait_recv()
            up_project(t - 2)

    loads[2].wait()
    down_tiles = [(pa, 0, ca), (pb, ca, cb)]

    def down(d):
        groups = near_y(d)
        h = jnp.concatenate([hidden[:, yi].reshape(NZ * rows, width) for yi in groups], axis=0)
        for dst, lo, size in down_tiles:
            half = size // 2

            def body(n, carry):
                w_at = pl.ds(pl.multiple_of(lo + n * half, 128), half)
                at = pl.ds(pl.multiple_of(n * half, 128), half)
                part = jnp.dot(h, down_w[:, w_at], preferred_element_type=F32)
                part = part.astype(BF16).reshape(len(groups), NZ, rows, half)
                for g, yi in enumerate(groups):
                    dst[:, yi, :, at] = part[g]
                return carry

            lax.fori_loop(0, 2, body, 0)

    sla, slb = scatter_line(LRA, pa, line_a), scatter_line(LRB, pb, line_b)
    sra = [scatter_ring(RA + slot, on_ring(pa, slot), ring_a.at[slot]) for slot in range(NZ)]
    srb = scatter_ring(RB, on_ring(pb, 0), ring_b)
    waits = (2, 1, 0, 1)

    def back_tick(ring, t):
        if 0 <= t < hops:
            ring[0](t)
        if t == hops:
            ring[1]()

    down(hops)
    for t in range(hops + 3):
        for slot in (2, 1, 3, 0):
            back_tick(sra[slot], t - waits[slot])
            if slot == 2 and t == hops:
                sla[0](FAR, 0, y).start()
            if slot == 1 and t == hops + 1:
                sla[1](0, y)
            if slot == 3 and t == hops + 1:
                sla[0](NEAR, 0, y).start()
        if t <= hops:
            for piece, yi in pieces(hops - t):
                slb[0](FAR, piece, yi).start()
        if 1 <= t <= hops + 1:
            for piece, yi in pieces(hops + 1 - t):
                slb[1](piece, yi)
        if t <= hops:
            for piece, yi in pieces(hops - t):
                slb[0](NEAR, piece, yi).start()
        if t < hops:
            down(hops - 1 - t)
        if t >= 2:
            for piece, yi in pieces(hops + 2 - t):
                slb[2](piece, yi)
            back_tick(srb, t - 2)
    sla[2](0, y)
    out[:, :ca] = pa[0, y]
    out[:, ca:] = pb[0, y]
    for kind in (FAR, RELAY, NEAR):
        gla(kind, 0, y).wait_send()
        sla[0](kind, 0, y).wait_send()
        for d in range(hops + 1):
            for piece, yi in pieces(d):
                glb(kind, piece, yi).wait_send()
                slb[0](kind, piece, yi).wait_send()
    for part in (*gra, grb, *sra, srb):
        part[2]()


def on_device(n_dp, n_tensor, tokens, norm_gain, gate_weight, up_weight, down_weight):
    rows, d = tokens.shape
    width = gate_weight.shape[1]
    ny = n_tensor // NZ
    hops = ny // 2
    ca = d // 16 * 7
    cb = d - ca
    vmem, anywhere = (pl.BlockSpec(memory_space=space) for space in (pltpu.VMEM, pl.ANY))
    dma = pltpu.SemaphoreType.DMA
    return pl.pallas_call(
        functools.partial(kernel, n_dp, ny),
        out_shape=jax.ShapeDtypeStruct((rows, d), BF16),
        in_specs=[vmem, vmem, anywhere, anywhere, anywhere],
        out_specs=vmem,
        scratch_shapes=[
            pltpu.VMEM((NZ, ny, rows, ca), BF16),
            pltpu.VMEM((NZ, ny, rows, cb), BF16),
            pltpu.VMEM((NZ, ny, rows, ca), BF16),
            pltpu.VMEM((NZ, ny, rows, cb), BF16),
            pltpu.VMEM((NZ, ny, rows, width), BF16),
            pltpu.VMEM((d, width), BF16),
            pltpu.VMEM((d, width), BF16),
            pltpu.VMEM((width, d), BF16),
            pltpu.VMEM((NZ, 2, 2, hops, rows, ca // 2), BF16),
            pltpu.VMEM((2, 2, hops, rows, cb // 2), BF16),
            pltpu.VMEM((3, 1, rows, ca), BF16),
            pltpu.VMEM((3, ny, rows, cb), BF16),
            dma((3,)),
            dma((10, 2, 2, hops)),
            dma((10, 2, 2, hops)),
            dma((4, 3, ny)),
            dma((4, 3, ny)),
        ],
        compiler_params=pltpu.CompilerParams(
            collective_id=0, has_side_effects=True, vmem_limit_bytes=60 * 1024 * 1024
        ),
    )(tokens, norm_gain.reshape(1, d), gate_weight, up_weight, down_weight)


def solution(mesh):
    return jax.shard_map(
        functools.partial(on_device, mesh.shape["dp"], mesh.shape["tensor"]),
        mesh=mesh,
        in_specs=(
            P(("dp", "tensor"), None),
            P(),
            P(None, "tensor"),
            P(None, "tensor"),
            P("tensor", None),
        ),
        out_specs=P(("dp", "tensor"), None),
        check_vma=False,
    )
```
